256 devices in a mesh: frames: 4 (over y_lo, core), lon: 64 (over y_hi, x, z).
Axes of the slice: x: 4, y: 4 (y_hi: 2, y_lo: 2; y = y_hi * 2 + y_lo), z: 8, core: 2. Of those that a mesh axis runs over, the one named last changes fastest.
Arguments:
- latents: bfloat16 [32, 2, 1024, 1024], P('frames', None, 'lon'), may hold values from -30 to 30
- window_weight: int32 [32, 64], P('frames'), may hold values from 1 to 8
- modulation: float32 [6, 1024], replicated, may hold values from -4 to 4
- query_spatial: bfloat16 [1024, 512], replicated, may hold values from -2 to 2, as said below
- key_spatial: bfloat16 [1024, 512], replicated, may hold values from -2 to 2, as said below
- value_spatial: bfloat16 [1024, 512], replicated, may hold values from -0.1875 to 0.1875
- out_spatial: bfloat16 [512, 1024], replicated, may hold values from -0.25 to 0.25
- query_temporal: bfloat16 [1024, 512], replicated, may hold values from -2 to 2, as said below
- key_temporal: bfloat16 [1024, 512], replicated, may hold values from -2 to 2, as said below
- value_temporal: bfloat16 [1024, 512], replicated, may hold values from -0.1875 to 0.1875
- out_temporal: bfloat16 [512, 1024], replicated, may hold values from -0.25 to 0.25
Outputs:
- block_output: bfloat16 [32, 2, 1024, 1024], P('frames', None, 'lon')
The draws below stay inside these ranges and needn't reach their ends.
Inputs may be any that keep to these rules, and one draw needn't show every extreme that they name: `query_spatial`: entries of a projection. `key_spatial`: entries of a projection. `query_temporal`: entries of a projection. `key_temporal`: entries of a projection.
All inputs are finite; a program needn't handle non-finite values.
Results may differ from the reference program's by a relative error of at most 0.0065.
Values may be sent and summed in bfloat16 or wider, within the bound.
No kernel may reach another device: no remote copies, remote signals or barrier semaphores. Data moves between devices by JAX's collectives and lax.ppermute only.
A program may use at most 64 MiB of HBM per device.

```python
import jax
import jax.numpy as jnp
from jax import lax

D = 1024
HEADS = 8
HD = 64
COLS = 16
F_DEV = 8
LAT = 2
HW = 512
FRAMES = 32
NCOL = 1024
NWIN = 64
N_FRAMES = 4


def draw_latents(key, part):
    base_draw = jax.random.normal(jax.random.fold_in(key, 1), (FRAMES, LAT, NCOL, D), jnp.float32)
    row_scale = jnp.exp(jax.random.uniform(jax.random.fold_in(key, 2), (FRAMES, LAT, NCOL, 1), jnp.float32, -0.6, 0.6))
    channel_scale = jnp.exp(jax.random.uniform(jax.random.fold_in(key, 3), (D,), jnp.float32, -0.6, 0.6))
    return (base_draw * row_scale * channel_scale).astype(jnp.bfloat16)


def paired_draw(key, salt):
    base_draw = jax.random.normal(jax.random.fold_in(key, salt), (D, HW), jnp.float32) * D ** (-0.5)
    other_draw = jax.random.normal(jax.random.fold_in(key, salt + 1), (D, HW), jnp.float32) * D ** (-0.5)
    return (base_draw, other_draw)


def draw_query_spatial(key, part):
    base_draw, other_draw = paired_draw(key, 10)
    return base_draw.astype(jnp.bfloat16)


def draw_key_spatial(key, part):
    base_draw, other_draw = paired_draw(key, 10)
    return other_draw.astype(jnp.bfloat16)


def draw_query_temporal(key, part):
    base_draw, other_draw = paired_draw(key, 20)
    return base_draw.astype(jnp.bfloat16)


def draw_key_temporal(key, part):
    base_draw, other_draw = paired_draw(key, 20)
    return other_draw.astype(jnp.bfloat16)


def plant(entries, rng, low, largest):
    longest = entries.shape.index(max(entries.shape))
    spots = []
    for shift in (0, 1):
        where = [jax.random.randint(jax.random.fold_in(rng, axis), (), 0, length) for axis, length in enumerate(entries.shape)]
        where[longest] = (where[longest] + shift) % entries.shape[longest]
        spots.append(tuple(where))
    return entries.at[spots[0]].set(low).at[spots[1]].set(largest)


def gaussian(key, extent, deviation, limit, dtype=jnp.bfloat16):
    array = deviation * jax.random.normal(key, extent, jnp.float32)
    return jnp.clip(array, min=-limit, max=limit).astype(dtype)


def setup_inputs(seed: int = 0) -> dict:
    seeds = jax.random.split(jax.random.key(seed), 12)
    latents = draw_latents(jax.random.fold_in(seeds[11], 71), 0)
    window_weight = plant(jax.random.randint(seeds[1], (FRAMES, NWIN), 1, 9), jax.random.fold_in(seeds[1], 1), 1, 8).astype(jnp.int32)
    modulation = gaussian(seeds[2], (6, D), 0.8, 4.0, jnp.float32)
    query_spatial = draw_query_spatial(jax.random.fold_in(seeds[11], 71), 0)
    key_spatial = draw_key_spatial(jax.random.fold_in(seeds[11], 71), 0)
    value_spatial = gaussian(seeds[5], (D, HW), D ** -0.5, 0.1875)
    out_spatial = gaussian(seeds[6], (HW, D), HW ** -0.5, 0.25)
    query_temporal = draw_query_temporal(jax.random.fold_in(seeds[11], 71), 0)
    key_temporal = draw_key_temporal(jax.random.fold_in(seeds[11], 71), 0)
    value_temporal = gaussian(seeds[9], (D, HW), D ** -0.5, 0.1875)
    out_temporal = gaussian(seeds[10], (HW, D), HW ** -0.5, 0.25)
    return dict(latents=latents, window_weight=window_weight, modulation=modulation, query_spatial=query_spatial, key_spatial=key_spatial, value_spatial=value_spatial, out_spatial=out_spatial, query_temporal=query_temporal, key_temporal=key_temporal, value_temporal=value_temporal, out_temporal=out_temporal)


EPSILON = 1e-06

def modulate(tokens, shift_row, scale_row):
    values = tokens.astype(jnp.float32)
    centre = lax.optimization_barrier(jnp.mean(values, axis=-1, keepdims=True))
    centred = values - centre
    spread = lax.optimization_barrier(jnp.mean(centred * centred, axis=-1, keepdims=True))
    normed = centred * lax.rsqrt(spread + EPSILON)
    return (normed * (1.0 + scale_row) + shift_row).astype(jnp.bfloat16)

def project(inputs, weight):
    return jnp.dot(inputs, weight, preferred_element_type=jnp.float32).astype(jnp.bfloat16)

def attend(queries, key_rows, values, score_form, mix_form):
    factor = queries.shape[-1] ** (-0.5)
    scores = jnp.einsum(score_form, queries.astype(jnp.float32), key_rows.astype(jnp.float32)) * factor
    maximum = lax.optimization_barrier(jnp.max(scores, axis=-1, keepdims=True))
    raised = jnp.exp(scores - maximum)
    attention = (raised / lax.optimization_barrier(jnp.sum(raised, axis=-1, keepdims=True))).astype(jnp.bfloat16)
    return jnp.einsum(mix_form, attention.astype(jnp.float32), values.astype(jnp.float32))

def reference(latents, window_weight, modulation, query_spatial, key_spatial, value_spatial, out_spatial, query_temporal, key_temporal, value_temporal, out_temporal):

    def window_rows(source):
        ahead_blocks = jnp.roll(source, -1, axis=1)
        joined = jnp.stack([source, ahead_blocks], axis=2)
        return jnp.transpose(joined, (1, 0, 2, 3, 4)).reshape(NWIN, LAT * 2 * COLS, HEADS, HD)

    def spatial_frame(inputs_pair):
        frame_tokens, weights_row = inputs_pair
        normed = modulate(frame_tokens, modulation[0], modulation[1])
        queries = project(normed, query_spatial).reshape(LAT, NWIN, COLS, HW)
        key_blocks = project(normed, key_spatial).reshape(LAT, NWIN, COLS, HW)
        value_blocks = project(normed, value_spatial).reshape(LAT, NWIN, COLS, HW)
        outputs = attend(window_rows(queries), window_rows(key_blocks), window_rows(value_blocks), 'bqhe,bkhe->bhqk', 'bhqk,bkhe->bqhe')
        outputs = outputs.reshape(NWIN, LAT, 2, COLS, HW)
        own_window = outputs[:, :, 0]
        prior_window = jnp.roll(outputs[:, :, 1], 1, axis=0)
        weight_here = weights_row.astype(jnp.float32)[:, None, None, None]
        weight_prior = jnp.roll(weights_row, 1).astype(jnp.float32)[:, None, None, None]
        blended = ((weight_here * own_window + weight_prior * prior_window) / (weight_here + weight_prior)).astype(jnp.bfloat16)
        blended = jnp.transpose(blended, (1, 0, 2, 3)).reshape(LAT, NCOL, HW)
        branch = jnp.dot(blended, out_spatial, preferred_element_type=jnp.float32)
        return (frame_tokens.astype(jnp.float32) + modulation[2] * branch).astype(jnp.bfloat16)
    mixed_tokens = lax.map(spatial_frame, (latents, window_weight))
    normed_time = modulate(mixed_tokens, modulation[3], modulation[4])
    tokens_all = LAT * NCOL

    def grouped(weight):
        values = project(normed_time, weight).reshape(N_FRAMES, F_DEV, tokens_all, HEADS, HD)
        return jnp.concatenate([values[:-1], values[1:]], axis=1)
    temporal = attend(grouped(query_temporal), grouped(key_temporal), grouped(value_temporal), 'gqnhe,gknhe->gnhqk', 'gnhqk,gknhe->gqnhe')
    temporal = temporal.reshape(N_FRAMES - 1, 2 * F_DEV, tokens_all, HW)
    padding = jnp.zeros((1, F_DEV, tokens_all, HW), jnp.float32)
    summed = jnp.concatenate([temporal[:, :F_DEV], padding], axis=0) + jnp.concatenate([padding, temporal[:, F_DEV:]], axis=0)
    position = jnp.arange(N_FRAMES)
    covers = 1.0 + ((position > 0) & (position < N_FRAMES - 1)).astype(jnp.float32)
    averaged = (summed / covers[:, None, None, None]).astype(jnp.bfloat16).reshape(FRAMES, LAT, NCOL, HW)
    branch = jnp.dot(averaged, out_temporal, preferred_element_type=jnp.float32)
    return (mixed_tokens.astype(jnp.float32) + modulation[5] * branch).astype(jnp.bfloat16)
```

```python
import functools

import jax
import jax.numpy as jnp
from jax import lax
from jax.experimental import pallas as pl
from jax.experimental.pallas import tpu as pltpu
from jax.sharding import PartitionSpec as P


HEADS = 8
HD = 64
D = 1024
HW = 512
F = 8
R = 2
C = 16
TOK = F * R * C
NCH = 2
FC = F // NCH
BLK = 128
EPSILON = 1e-06
NEG = -1e30
MIB = 1024 * 1024


VM = pl.BlockSpec(memory_space=pltpu.VMEM)
HBM = pl.BlockSpec(memory_space=pltpu.HBM)


def f32dot(a, b):
    return jnp.dot(a, b, preferred_element_type=jnp.float32)


def modulate(values, shift_row, scale_row):
    centre = jnp.mean(values, axis=-1, keepdims=True)
    centred = values - centre
    spread = jnp.mean(centred * centred, axis=-1, keepdims=True)
    normed = centred * lax.rsqrt(spread + EPSILON)
    return (normed * (1.0 + scale_row) + shift_row).astype(jnp.bfloat16)


def mixed_heads(q, keys, values, bias, share_a, share_b):
    half = lax.broadcasted_iota(jnp.int32, (BLK, BLK), 1) < HD
    zero = jnp.zeros((BLK, BLK), jnp.bfloat16)
    ones = jnp.ones((2 * BLK, BLK), jnp.bfloat16)
    pieces = []
    for pair in range(HEADS // 2):
        lanes = slice(pair * BLK, (pair + 1) * BLK)
        qp = q[:, lanes]
        stacked = jnp.concatenate([jnp.where(half, qp, zero), jnp.where(half, zero, qp)], axis=0)
        kc = jnp.concatenate([k[:, lanes] for k in keys], axis=0)
        scores = lax.dot_general(
            stacked, kc, (((1,), (1,)), ((), ())), preferred_element_type=jnp.float32
        )
        scores = scores + bias
        total = None
        for first, share in ((0, share_a), (1, share_b)):
            window = scores[:, first * BLK : (first + 2) * BLK]
            top = jnp.max(window, axis=-1, keepdims=True)
            raised = jnp.exp(window - top).astype(jnp.bfloat16)
            vc = jnp.concatenate([values[first][:, lanes], values[first + 1][:, lanes]], axis=0)
            mix = f32dot(raised, jnp.concatenate([vc, ones], axis=1))
            part = mix[:, :BLK] * (share / mix[:, BLK:])
            total = part if total is None else total + part
        pieces.append(jnp.where(half, total[:BLK], total[BLK:]))
    return jnp.concatenate(pieces, axis=1).astype(jnp.bfloat16)


def block_bias(key_of):
    row = lax.broadcasted_iota(jnp.int32, (2 * BLK, 3 * BLK), 0)
    col = lax.broadcasted_iota(jnp.int32, (2 * BLK, 3 * BLK), 1)
    return jnp.where(key_of(row) == key_of(col), 0.0, NEG)


def frame_shares(weight_ref, frame):
    count = weight_ref.shape[1]
    strip = lax.axis_index("lon")
    weights = weight_ref[...].astype(jnp.float32)
    spot = lax.broadcasted_iota(jnp.int32, weights.shape, 1)
    here = jnp.sum(jnp.where(spot == strip, weights, 0.0), axis=1, keepdims=True)
    prior = jnp.sum(
        jnp.where(spot == lax.rem(strip + count - 1, count), weights, 0.0), axis=1, keepdims=True
    )
    share = here / (here + prior)
    rows = [
        jnp.broadcast_to(share[f : f + 1], (R * C, 1))
        for f in range(frame, frame + BLK // (R * C))
    ]
    return jnp.concatenate(rows + rows, axis=0)


def own_kernel(*refs):
    mod_ref, x_hbm, wq_hbm = refs[:3]
    stored_hbm = refs[3:10]
    x_ref, q_ref, k_ref, v_ref = refs[10:14]
    stored = refs[14:21]
    wq_ref, sem = refs[21:]
    copies = [
        pltpu.make_async_copy(src, dst, sem.at[i])
        for i, (src, dst) in enumerate(
            zip((x_hbm, wq_hbm) + stored_hbm, (x_ref, wq_ref) + stored)
        )
    ]
    for copy in copies:
        copy.start()
    copies[0].wait()
    blocks = [slice(i * BLK, (i + 1) * BLK) for i in range(TOK // BLK)]
    normed = [
        modulate(x_ref[rows].astype(jnp.float32), mod_ref[0:1], mod_ref[1:2]) for rows in blocks
    ]
    copies[1].wait()
    for rows, n in zip(blocks, normed):
        q_ref[rows] = (f32dot(n, wq_ref[...]).astype(jnp.bfloat16) * HD**-0.5).astype(jnp.bfloat16)
    copies[2].wait()
    for rows, n in zip(blocks, normed):
        k_ref[rows] = f32dot(n, stored[0][...]).astype(jnp.bfloat16)
    copies[3].wait()
    for rows, n in zip(blocks, normed):
        v_ref[rows] = f32dot(n, stored[1][...]).astype(jnp.bfloat16)
    for copy in copies[4:]:
        copy.wait()


def split_kernel(x_hbm, *refs):
    sem = refs[-1]
    rows = TOK // NCH
    copies = [
        pltpu.make_async_copy(x_hbm.at[pl.ds(i * rows, rows)], refs[i], sem.at[i])
        for i in range(NCH)
    ]
    for copy in copies:
        copy.start()
    for copy in copies:
        copy.wait()


def space_kernel(
    base,
    west_ref,
    east_ref,
    x_ref,
    q_ref,
    k_ref,
    v_ref,
    weight_ref,
    mod_ref,
    wk_ref,
    wv_ref,
    wo_ref,
    wqt_ref,
    wkt_ref,
    wvt_ref,
    mixed_ref,
    qt_ref,
    kvt_ref,
):
    bias = block_bias(lambda i: (i & (BLK - 1)) >> 5)
    for i in range(west_ref.shape[0] // BLK):
        here = slice(i * BLK, (i + 1) * BLK)
        rows = slice(base + i * BLK, base + (i + 1) * BLK)
        sides = []
        for ref in (west_ref, east_ref):
            n = modulate(ref[here].astype(jnp.float32), mod_ref[0:1], mod_ref[1:2])
            sides.append(
                (
                    f32dot(n, wk_ref[...]).astype(jnp.bfloat16),
                    f32dot(n, wv_ref[...]).astype(jnp.bfloat16),
                )
            )
        share = frame_shares(weight_ref, (base + i * BLK) // (R * C))
        blended = mixed_heads(
            q_ref[rows],
            (sides[0][0], k_ref[rows], sides[1][0]),
            (sides[0][1], v_ref[rows], sides[1][1]),
            bias,
            1.0 - share,
            share,
        )
        branch = f32dot(blended, wo_ref[...])
        mixed = (x_ref[rows].astype(jnp.float32) + mod_ref[2:3] * branch).astype(jnp.bfloat16)
        mixed_ref[here] = mixed
        n = modulate(mixed.astype(jnp.float32), mod_ref[3:4], mod_ref[4:5])
        kvt_ref[here, :HW] = f32dot(n, wkt_ref[...]).astype(jnp.bfloat16)
        kvt_ref[here, HW:] = f32dot(n, wvt_ref[...]).astype(jnp.bfloat16)
        qt_ref[here] = (f32dot(n, wqt_ref[...]).astype(jnp.bfloat16) * HD**-0.5).astype(
            jnp.bfloat16
        )


def time_kernel(*refs):
    mod_ref, wo_ref = refs[:2]
    chunks = [refs[2 + 5 * i : 7 + 5 * i] for i in range(NCH)]
    group = lax.axis_index("frames")
    paired = jnp.where(
        jnp.logical_and(group > 0, group < lax.axis_size("frames") - 1), 0.5, 0.0
    )
    out_ref = refs[-1]
    bias = block_bias(lambda i: i & (C - 1))
    for r in range(R):

        def rows_of(slot, lanes):
            return jnp.concatenate(
                [
                    refs_here[slot][f * R * C + r * C : f * R * C + (r + 1) * C, lanes]
                    for refs_here in chunks
                    for f in range(FC)
                ],
                axis=0,
            )

        first, second, whole = slice(0, HW), slice(HW, 2 * HW), slice(0, D)
        blended = mixed_heads(
            rows_of(0, first),
            (rows_of(2, first), rows_of(1, first), rows_of(3, first)),
            (rows_of(2, second), rows_of(1, second), rows_of(3, second)),
            bias,
            1.0 - paired,
            paired,
        )
        branch = f32dot(blended, wo_ref[...])
        out = (rows_of(4, whole).astype(jnp.float32) + mod_ref[5:6] * branch).astype(jnp.bfloat16)
        for f in range(F):
            out_ref[f * R * C + r * C : f * R * C + (r + 1) * C] = out[f * C : (f + 1) * C]


def body(
    latents,
    window_weight,
    modulation,
    query_spatial,
    key_spatial,
    value_spatial,
    out_spatial,
    query_temporal,
    key_temporal,
    value_temporal,
    out_temporal,
):
    strips = lax.axis_size("lon")
    bf = jnp.bfloat16
    x = latents.reshape(TOK, D)
    rows = TOK // NCH
    forward = [(i, (i + 1) % strips) for i in range(strips)]
    back = [((i + 1) % strips, i) for i in range(strips)]
    shape = jax.ShapeDtypeStruct

    def keep(array):
        return pltpu.with_memory_space_constraint(array, pltpu.HBM)

    if NCH > 1:
        chunks = pl.pallas_call(
            split_kernel,
            out_shape=[shape((rows, D), bf)] * NCH,
            in_specs=[HBM],
            out_specs=[VM] * NCH,
            scratch_shapes=[pltpu.SemaphoreType.DMA((NCH,))],
            compiler_params=pltpu.CompilerParams(vmem_limit_bytes=4 * MIB),
            name="split",
        )(keep(x))
    else:
        chunks = [x]
    west, east = [], []
    for i in range(NCH):
        west.append(lax.ppermute(chunks[i], "lon", forward))
    for i in range(NCH):
        east.append(lax.ppermute(chunks[i], "lon", back))

    wide, tall = shape((D, HW), bf), shape((HW, D), bf)
    stored = pl.pallas_call(
        own_kernel,
        out_shape=[shape((TOK, D), bf)]
        + [shape((TOK, HW), bf)] * 3
        + [wide, wide, tall, wide, wide, wide, tall],
        in_specs=[VM] + [HBM] * 9,
        out_specs=[VM] * 11,
        scratch_shapes=[pltpu.VMEM((D, HW), bf), pltpu.SemaphoreType.DMA((9,))],
        compiler_params=pltpu.CompilerParams(vmem_limit_bytes=24 * MIB),
        name="own",
    )(
        modulation,
        *map(
            keep,
            (
                x,
                query_spatial,
                key_spatial,
                value_spatial,
                out_spatial,
                query_temporal,
                key_temporal,
                value_temporal,
                out_temporal,
            ),
        ),
    )
    own, weights, out_weight = stored[:4], stored[4:10], stored[10]
    time_args = []
    for i in range(NCH):
        mixed, qt, kvt = pl.pallas_call(
            functools.partial(space_kernel, i * rows),
            out_shape=[shape((rows, D), bf), shape((rows, HW), bf), shape((rows, D), bf)],
            in_specs=[VM] * 14,
            out_specs=[VM] * 3,
            compiler_params=pltpu.CompilerParams(vmem_limit_bytes=20 * MIB),
        )(west[i], east[i], *own, window_weight, modulation, *weights)
        cross = lax.ppermute(kvt, "frames", [(1, 2), (2, 1)])
        mate = lax.ppermute(kvt, "frames", [(0, 1), (1, 0), (2, 3), (3, 2)])
        time_args += [qt, kvt, mate, cross, mixed]

    out = pl.pallas_call(
        time_kernel,
        out_shape=shape((TOK, D), bf),
        in_specs=[VM] * (2 + len(time_args)),
        out_specs=VM,
        compiler_params=pltpu.CompilerParams(vmem_limit_bytes=20 * MIB),
        name="time",
    )(modulation, out_weight, *time_args)
    return out.reshape(latents.shape)


def solution(mesh):
    return jax.shard_map(
        body,
        mesh=mesh,
        in_specs=(P("frames", None, "lon", None), P("frames", None)) + (P(),) * 9,
        out_specs=P("frames", None, "lon", None),
        check_vma=False,
    )
```

```python
import functools

import jax
import jax.numpy as jnp
from jax import lax
from jax.experimental import pallas as pl
from jax.experimental.pallas import tpu as pltpu
from jax.sharding import PartitionSpec as P


HEADS = 8
HD = 64
D = 1024
HW = 512
F = 8
SPOTS = 32
TOK = F * SPOTS
PIECES = (5, 3)
STARTS = tuple(sum(PIECES[:i]) for i in range(len(PIECES)))
GROUP = 8
GROUPS = SPOTS // GROUP
LANES = 128
TOGETHER = 16
SPACE_TOGETHER = 16
AHEAD = True
PAD = True
EPSILON = 1e-06
NEG = -1e30
MIB = 1024 * 1024


VM = pl.BlockSpec(memory_space=pltpu.VMEM)
HBM = pl.BlockSpec(memory_space=pltpu.HBM)


def f32dot(a, b):
    return jnp.dot(a, b, preferred_element_type=jnp.float32)


def project(a, w_ref):
    return f32dot(a, w_ref[...]).astype(jnp.bfloat16)


def scaled(q):
    return (q * HD**-0.5).astype(jnp.bfloat16)


def normed(values, shift_row, scale_row):
    centre = jnp.mean(values, axis=-1, keepdims=True)
    centred = values - centre
    spread = jnp.mean(centred * centred, axis=-1, keepdims=True)
    return (centred * lax.rsqrt(spread + EPSILON)) * (1.0 + scale_row) + shift_row


def spread_heads(q, count):
    head = lax.broadcasted_iota(jnp.int32, q.shape, 1) // HD
    zero = jnp.zeros_like(q)
    return jnp.concatenate([jnp.where(head == h, q, zero) for h in range(count)], axis=0)


def gather_heads(o, rows, count):
    tiles = []
    half = lax.broadcasted_iota(jnp.int32, (rows, LANES), 1) < HD
    for tile in range(count * HD // LANES):
        lanes = slice(tile * LANES, (tile + 1) * LANES)
        even = o[2 * tile * rows : (2 * tile + 1) * rows, lanes]
        odd = o[(2 * tile + 1) * rows : (2 * tile + 2) * rows, lanes]
        tiles.append(jnp.where(half, even, odd))
    return tiles[0] if len(tiles) == 1 else jnp.concatenate(tiles, axis=1)


def raise_scores(keys, stacked, n, bias=None):
    scores = lax.dot_general(
        keys, stacked, (((1,), (1,)), ((), ())), preferred_element_type=jnp.float32
    )
    out = []
    for i in range(keys.shape[0] // n):
        part = scores[i * n : (i + 1) * n]
        if bias is not None:
            part = part + bias
        top = jnp.max(part, axis=0, keepdims=True)
        raised = jnp.exp(part - top)
        out.append((raised, top, jnp.sum(raised, axis=0, keepdims=True)))
    return out


def window_factors(share, first, second):
    high = jnp.maximum(first[0], second[0])
    a, b = jnp.exp(first[0] - high), jnp.exp(second[0] - high)
    scale = share / (first[1] * a + second[1] * b)
    return a * scale, b * scale


def mix_values(raised, factors, values, rows, count):
    weights = jnp.concatenate(
        [(part * factor).astype(jnp.bfloat16) for part, factor in zip(raised, factors)], axis=0
    )
    mix = lax.dot_general(
        weights,
        jnp.concatenate(values, axis=0),
        (((0,), (0,)), ((), ())),
        preferred_element_type=jnp.float32,
    )
    return gather_heads(mix, rows, count)


def split_kernel(x_ref, *refs):
    for ref, start, frames in zip(refs, STARTS, PIECES):
        ref[...] = x_ref[start * SPOTS : (start + frames) * SPOTS]


def own_kernel(*refs):
    mod_ref, weight_ref, x_hbm, wq_hbm = refs[:4]
    stored_hbm = refs[4:11]
    share_ref, x_ref, q_ref, kv_ref = refs[11:15]
    stored = refs[15:22]
    wq_ref, sem = refs[22:]
    copies = [
        pltpu.make_async_copy(src, dst, sem.at[i])
        for i, (src, dst) in enumerate(
            zip((x_hbm, wq_hbm) + stored_hbm, (x_ref, wq_ref) + stored)
        )
    ]
    for copy in copies:
        copy.start()

    count = weight_ref.shape[1]
    strip = lax.axis_index("lon")
    weights = weight_ref[...].astype(jnp.float32)
    spot = lax.broadcasted_iota(jnp.int32, weights.shape, 1)
    here = jnp.sum(jnp.where(spot == strip, weights, 0.0), axis=1, keepdims=True)
    prior = jnp.sum(
        jnp.where(spot == lax.rem(strip + count - 1, count), weights, 0.0), axis=1, keepdims=True
    )
    near = jnp.where(lax.rem(strip, 2) == 0, here, prior)
    share_ref[...] = jnp.broadcast_to(near / (here + prior), share_ref.shape)

    copies[0].wait()
    n = normed(x_ref[...].astype(jnp.float32), mod_ref[0:1], mod_ref[1:2]).astype(jnp.bfloat16)
    copies[1].wait()
    q_ref[...] = scaled(project(n, wq_ref))
    for i in range(2):
        copies[2 + i].wait()
        kv_ref[:, i * HW : (i + 1) * HW] = project(n, stored[i])
    for copy in copies[4:]:
        copy.wait()


def quad_lanes(quad):
    wide = HW // 2
    return slice(quad * wide, (quad + 1) * wide), slice(HW + quad * wide, HW + (quad + 1) * wide)


def frame_rows(f):
    return slice(f * SPOTS, (f + 1) * SPOTS)


def near_kernel(x_ref, share_ref, q_ref, kv_ref, mod_ref, wk_ref, wv_ref, part_ref, raised_ref, stats_ref):
    n = normed(x_ref[...].astype(jnp.float32), mod_ref[0:1], mod_ref[1:2]).astype(jnp.bfloat16)
    k_near, v_near = project(n, wk_ref), project(n, wv_ref)
    units = [(f, quad) for f in range(F) for quad in range(2)]
    for first in range(0, len(units), SPACE_TOGETHER):
        batch = units[first : first + SPACE_TOGETHER]
        scored = []
        for f, quad in batch:
            lanes, after = quad_lanes(quad)
            at = frame_rows(f)
            keys = jnp.concatenate([kv_ref[at, lanes], k_near[at, lanes]], axis=0)
            stacked = spread_heads(q_ref[at, lanes], HEADS // 2)
            scored.append(raise_scores(keys, stacked, SPOTS))
        for (f, quad), (own, other) in zip(batch, scored):
            lanes, after = quad_lanes(quad)
            at = frame_rows(f)
            unit = 2 * f + quad
            raised_ref[unit] = own[0]
            stats_ref[unit, 0:1] = own[1]
            stats_ref[unit, 1:2] = own[2]
            part_ref[at, lanes] = mix_values(
                [own[0], other[0]],
                window_factors(share_ref[f : f + 1], own[1:], other[1:]),
                [kv_ref[at, after], v_near[at, lanes]],
                SPOTS,
                HEADS // 2,
            )


def space_kernel(start, frames, *refs):
    far_ref, part_ref, raised_ref, stats_ref, share_ref, x_ref, q_ref, kv_ref = refs[:8]
    mod_ref, wk_ref, wv_ref, wo_ref, wkt_ref, wvt_ref = refs[8:14]
    mixed_ref, n_ref, kvt_ref = refs[14:]
    rows = frames * SPOTS
    far = far_ref[...]
    if PAD and rows < LANES:
        far = jnp.concatenate([far, far[: LANES - rows]], axis=0)
    n = normed(far.astype(jnp.float32), mod_ref[0:1], mod_ref[1:2]).astype(jnp.bfloat16)
    k_far, v_far = project(n, wk_ref), project(n, wv_ref)
    units = [(f, quad) for f in range(frames) for quad in range(2)]
    blended = {}
    for first in range(0, len(units), SPACE_TOGETHER):
        batch = units[first : first + SPACE_TOGETHER]
        scored = []
        for f, quad in batch:
            lanes, after = quad_lanes(quad)
            stacked = spread_heads(q_ref[frame_rows(start + f), lanes], HEADS // 2)
            scored += raise_scores(k_far[frame_rows(f), lanes], stacked, SPOTS)
        for (f, quad), other in zip(batch, scored):
            lanes, after = quad_lanes(quad)
            own = frame_rows(start + f)
            unit = 2 * (start + f) + quad
            stats = (stats_ref[unit, 0:1], stats_ref[unit, 1:2])
            share = 1.0 - share_ref[start + f : start + f + 1]
            mix = mix_values(
                [raised_ref[unit], other[0]],
                window_factors(share, stats, other[1:]),
                [kv_ref[own, after], v_far[frame_rows(f), lanes]],
                SPOTS,
                HEADS // 2,
            )
            blended[f, quad] = (part_ref[own, lanes] + mix).astype(jnp.bfloat16)
    blended = jnp.concatenate(
        [
            jnp.concatenate([blended[f, quad] for quad in range(2)], axis=1)
            for f in range(frames)
        ],
        axis=0,
    )
    here = slice(start * SPOTS, (start + frames) * SPOTS)
    branch = f32dot(blended, wo_ref[...])
    mixed = (x_ref[here].astype(jnp.float32) + mod_ref[2:3] * branch).astype(jnp.bfloat16)
    mixed_ref[...] = mixed
    n = normed(mixed.astype(jnp.float32), mod_ref[3:4], mod_ref[4:5])
    n = n.reshape(frames, GROUPS, GROUP, D).transpose(1, 0, 2, 3).reshape(rows, D)
    n = n.astype(jnp.bfloat16)
    kvt_ref[:, :HW] = project(n, wkt_ref)
    kvt_ref[:, HW:] = project(n, wvt_ref)
    n_ref[...] = n


def time_setup():
    rows = F * GROUP
    key_spot = lax.broadcasted_iota(jnp.int32, (rows, LANES), 0) % GROUP
    query_spot = lax.broadcasted_iota(jnp.int32, (rows, LANES), 1) % GROUP
    bias = jnp.where(key_spot == query_spot, 0.0, NEG)
    group = lax.axis_index("frames")
    inner = jnp.logical_and(group > 0, group < lax.axis_size("frames") - 1)
    return bias, jnp.where(inner, 0.5, 0.0)


def rows_of(refs, g, lanes):
    return jnp.concatenate(
        [
            ref[g * frames * GROUP : (g + 1) * frames * GROUP, lanes]
            for ref, frames in zip(refs, PIECES)
        ],
        axis=0,
    )


def pair_lanes(pair):
    return slice(pair * LANES, (pair + 1) * LANES), slice(
        HW + pair * LANES, HW + (pair + 1) * LANES
    )


def mate_kernel(*refs):
    count = len(PIECES)
    wq_ref = refs[0]
    n_refs, own_refs, mate_refs = (refs[1 + i * count : 1 + (i + 1) * count] for i in range(3))
    q_ref, part_ref, raised_ref, stats_ref = refs[1 + 3 * count :]
    bias, paired = time_setup()
    n = F * GROUP
    q = scaled(project(jnp.concatenate([ref[...] for ref in n_refs], axis=0), wq_ref))
    for g in range(GROUPS):
        q_ref[g * n : (g + 1) * n] = jnp.concatenate(
            [
                q[start * SPOTS + g * frames * GROUP : start * SPOTS + (g + 1) * frames * GROUP]
                for start, frames in zip(STARTS, PIECES)
            ],
            axis=0,
        )
    units = [(g, pair) for g in range(GROUPS) for pair in range(HEADS // 2)]
    for first in range(0, len(units), TOGETHER):
        batch = units[first : first + TOGETHER]
        scored = []
        for g, pair in batch:
            lanes, after = pair_lanes(pair)
            stacked = spread_heads(q_ref[g * n : (g + 1) * n, lanes], 2)
            keys = jnp.concatenate(
                [rows_of(own_refs, g, lanes), rows_of(mate_refs, g, lanes)], axis=0
            )
            scored.append(raise_scores(keys, stacked, n, bias))
        for (g, pair), (own, other) in zip(batch, scored):
            lanes, after = pair_lanes(pair)
            unit = g * (HEADS // 2) + pair
            raised_ref[unit] = own[0]
            stats_ref[unit, 0:1] = own[1]
            stats_ref[unit, 1:2] = own[2]
            part_ref[g * n : (g + 1) * n, lanes] = mix_values(
                [own[0], other[0]],
                window_factors(1.0 - paired, own[1:], other[1:]),
                [rows_of(own_refs, g, after), rows_of(mate_refs, g, after)],
                n,
                2,
            )


def cross_kernel(mod_ref, wo_ref, q_ref, part_ref, raised_ref, stats_ref, *refs):
    count = len(PIECES)
    own_refs, cross_refs, mixed_refs = (refs[i * count : (i + 1) * count] for i in range(3))
    out_hbm, out_ref, sem = refs[3 * count :]
    bias, paired = time_setup()
    n = F * GROUP
    copies = []
    per = GROUPS // 2
    pairs = range(HEADS // 2)

    def score(half):
        scored = {}
        for g in range(half * per, (half + 1) * per):
            for pair in pairs:
                lanes, _ = pair_lanes(pair)
                stacked = spread_heads(q_ref[g * n : (g + 1) * n, lanes], 2)
                scored[g, pair] = raise_scores(rows_of(cross_refs, g, lanes), stacked, n, bias)[0]
        return scored

    scored = {}
    if AHEAD:
        for half in range(2):
            scored.update(score(half))
    for half in range(2):
        if not AHEAD:
            scored = score(half)
        rows = []
        for g in range(half * per, (half + 1) * per):
            row = []
            for pair in pairs:
                lanes, after = pair_lanes(pair)
                unit = g * (HEADS // 2) + pair
                other = scored[g, pair]
                stats = (stats_ref[unit, 0:1], stats_ref[unit, 1:2])
                mix = mix_values(
                    [raised_ref[unit], other[0]],
                    window_factors(paired, stats, other[1:]),
                    [rows_of(own_refs, g, after), rows_of(cross_refs, g, after)],
                    n,
                    2,
                )
                row.append((part_ref[g * n : (g + 1) * n, lanes] + mix).astype(jnp.bfloat16))
            rows.append(jnp.concatenate(row, axis=1))
        branch = mod_ref[5:6] * f32dot(jnp.concatenate(rows, axis=0), wo_ref[...])
        branch = branch.reshape(per, F, GROUP, D)
        spots = pl.ds(half * per, per)
        for mixed_ref, start, frames in zip(mixed_refs, STARTS, PIECES):
            for f in range(frames):
                for i in range(per):
                    at = f * SPOTS + (half * per + i) * GROUP
                    mixed = mixed_ref[at : at + GROUP].astype(jnp.float32)
                    out_ref[start + f, half * per + i] = (mixed + branch[i, start + f]).astype(
                        jnp.bfloat16
                    )
        for f in range(0, F, 2):
            pick = pl.ds(f, 2)
            copies.append(
                pltpu.make_async_copy(
                    out_ref.at[pick, spots], out_hbm.at[pick, spots], sem.at[half * F + f]
                )
            )
            copies[-1].start()
    for copy in copies:
        copy.wait()


def body(
    latents,
    window_weight,
    modulation,
    query_spatial,
    key_spatial,
    value_spatial,
    out_spatial,
    query_temporal,
    key_temporal,
    value_temporal,
    out_temporal,
):
    strips = lax.axis_size("lon")
    groups = lax.axis_size("frames")
    bf = jnp.bfloat16
    shape = jax.ShapeDtypeStruct
    params = pltpu.CompilerParams

    def keep(array):
        return pltpu.with_memory_space_constraint(array, pltpu.HBM)

    x = latents.reshape(TOK, D)
    near_pairs = [(i, i ^ 1) for i in range(strips)]
    far_pairs = [(i, (i + (1 if i % 2 else -1)) % strips) for i in range(strips)]
    mates = [(i, i ^ 1) for i in range(groups)]
    crossing = []
    for i in range(groups):
        for s in range(strips):
            if i in (0, groups - 1):
                crossing.append((i * strips + s, i * strips + (s ^ 1)))
            else:
                partner = i + 1 if i % 2 else i - 1
                crossing.append((i * strips + s, partner * strips + s))

    near = lax.ppermute(x, "lon", near_pairs)
    pieces = pl.pallas_call(
        split_kernel,
        out_shape=[shape((n * SPOTS, D), bf) for n in PIECES],
        in_specs=[VM],
        out_specs=[VM] * len(PIECES),
        compiler_params=params(vmem_limit_bytes=4 * MIB),
        name="split",
    )(x)
    far = []
    for piece in pieces:
        far.append(lax.ppermute(piece, "lon", far_pairs))

    wide, tall = shape((D, HW), bf), shape((HW, D), bf)
    stored = pl.pallas_call(
        own_kernel,
        out_shape=[shape((F, LANES), jnp.float32), shape((TOK, D), bf)]
        + [shape((TOK, HW), bf), shape((TOK, D), bf)]
        + [wide, wide, tall, wide, wide, wide, tall],
        in_specs=[VM] * 2 + [HBM] * 9,
        out_specs=[VM] * 11,
        scratch_shapes=[pltpu.VMEM((D, HW), bf), pltpu.SemaphoreType.DMA((9,))],
        compiler_params=params(vmem_limit_bytes=24 * MIB),
        name="own",
    )(
        modulation,
        window_weight,
        *map(
            keep,
            (
                x,
                query_spatial,
                key_spatial,
                value_spatial,
                out_spatial,
                key_temporal,
                value_temporal,
                query_temporal,
                out_temporal,
            ),
        ),
    )
    share, own_x, q, kv = stored[:4]
    weights = stored[4:9]
    space_units = 2 * F
    near_parts = pl.pallas_call(
        near_kernel,
        out_shape=[
            shape((TOK, HW), jnp.float32),
            shape((space_units, SPOTS, LANES), jnp.float32),
            shape((space_units, 8, LANES), jnp.float32),
        ],
        in_specs=[VM] * 7,
        out_specs=[VM] * 3,
        compiler_params=params(vmem_limit_bytes=16 * MIB),
        name="near",
    )(near, share, q, kv, modulation, *weights[:2])
    time_args = []
    for i, (start, frames) in enumerate(zip(STARTS, PIECES)):
        rows = frames * SPOTS
        args = (far[i], *near_parts, share, own_x, q, kv, modulation, *weights)
        mixed, nt, kvt = pl.pallas_call(
            functools.partial(space_kernel, start, frames),
            out_shape=[shape((rows, D), bf)] * 3,
            in_specs=[VM] * len(args),
            out_specs=[VM] * 3,
            compiler_params=params(vmem_limit_bytes=20 * MIB),
        )(*args)
        cross = lax.ppermute(kvt, ("frames", "lon"), crossing)
        mate = lax.ppermute(kvt, "frames", mates)
        time_args.append((nt, kvt, mate, cross, mixed))

    nts, kvts, mate_kvs, cross_kvs, mixeds = zip(*time_args)
    units = GROUPS * HEADS // 2
    parts = pl.pallas_call(
        mate_kernel,
        out_shape=[
            shape((TOK, HW), bf),
            shape((TOK, HW), jnp.float32),
            shape((units, F * GROUP, LANES), jnp.float32),
            shape((units, 8, LANES), jnp.float32),
        ],
        in_specs=[VM] * (1 + 3 * len(PIECES)),
        out_specs=[VM] * 4,
        compiler_params=params(vmem_limit_bytes=12 * MIB),
        name="timea",
    )(stored[9], *nts, *kvts, *mate_kvs)
    out_shape = (F, GROUPS, GROUP, D)
    out = pl.pallas_call(
        cross_kernel,
        out_shape=shape(out_shape, bf),
        in_specs=[VM] * (6 + 3 * len(PIECES)),
        out_specs=HBM,
        scratch_shapes=[pltpu.VMEM(out_shape, bf), pltpu.SemaphoreType.DMA((2 * F,))],
        compiler_params=params(vmem_limit_bytes=16 * MIB),
        name="timeb",
    )(modulation, stored[10], *parts, *kvts, *cross_kvs, *mixeds)
    return out.reshape(latents.shape)


def solution(mesh):
    return jax.shard_map(
        body,
        mesh=mesh,
        in_specs=(P("frames", None, "lon", None), P("frames", None)) + (P(),) * 9,
        out_specs=P("frames", None, "lon", None),
        check_vma=False,
    )
```

```python
import functools

import jax
import jax.numpy as jnp
from jax import lax
from jax.experimental import pallas as pl
from jax.experimental.pallas import tpu as pltpu
from jax.sharding import PartitionSpec as P


HEADS = 8
HD = 64
D = 1024
HW = 512
F = 8
SPOTS = 32
TOK = F * SPOTS
PIECES = (5, 3)
STARTS = tuple(sum(PIECES[:i]) for i in range(len(PIECES)))
GROUP = 8
GROUPS = SPOTS // GROUP
LANES = 128
TOGETHER = 16
SPACE_TOGETHER = 16
AHEAD = True
PAD = True
EPSILON = 1e-06
NEG = -1e30
MIB = 1024 * 1024


VM = pl.BlockSpec(memory_space=pltpu.VMEM)
HBM = pl.BlockSpec(memory_space=pltpu.HBM)


def f32dot(a, b):
    return jnp.dot(a, b, preferred_element_type=jnp.float32)


def project(a, w_ref):
    return f32dot(a, w_ref[...]).astype(jnp.bfloat16)


def scaled(q):
    return (q * HD**-0.5).astype(jnp.bfloat16)


def normed(values, shift_row, scale_row):
    centre = jnp.mean(values, axis=-1, keepdims=True)
    centred = values - centre
    spread = jnp.mean(centred * centred, axis=-1, keepdims=True)
    return (centred * lax.rsqrt(spread + EPSILON)) * (1.0 + scale_row) + shift_row


def spread_heads(q, count):
    head = lax.broadcasted_iota(jnp.int32, q.shape, 1) // HD
    zero = jnp.zeros_like(q)
    return jnp.concatenate([jnp.where(head == h, q, zero) for h in range(count)], axis=0)


def gather_heads(o, rows, count):
    tiles = []
    half = lax.broadcasted_iota(jnp.int32, (rows, LANES), 1) < HD
    for tile in range(count * HD // LANES):
        lanes = slice(tile * LANES, (tile + 1) * LANES)
        even = o[2 * tile * rows : (2 * tile + 1) * rows, lanes]
        odd = o[(2 * tile + 1) * rows : (2 * tile + 2) * rows, lanes]
        tiles.append(jnp.where(half, even, odd))
    return tiles[0] if len(tiles) == 1 else jnp.concatenate(tiles, axis=1)


def raise_scores(keys, stacked, n, bias=None):
    scores = lax.dot_general(
        keys, stacked, (((1,), (1,)), ((), ())), preferred_element_type=jnp.float32
    )
    out = []
    for i in range(keys.shape[0] // n):
        part = scores[i * n : (i + 1) * n]
        if bias is not None:
            part = part + bias
        top = jnp.max(part, axis=0, keepdims=True)
        raised = jnp.exp(part - top)
        out.append((raised, top, jnp.sum(raised, axis=0, keepdims=True)))
    return out


def window_factors(share, first, second):
    high = jnp.maximum(first[0], second[0])
    a, b = jnp.exp(first[0] - high), jnp.exp(second[0] - high)
    scale = share / (first[1] * a + second[1] * b)
    return a * scale, b * scale


def mix_values(raised, factors, values, rows, count):
    weights = jnp.concatenate(
        [(part * factor).astype(jnp.bfloat16) for part, factor in zip(raised, factors)], axis=0
    )
    mix = lax.dot_general(
        weights,
        jnp.concatenate(values, axis=0),
        (((0,), (0,)), ((), ())),
        preferred_element_type=jnp.float32,
    )
    return gather_heads(mix, rows, count)


def split_kernel(x_ref, *refs):
    for ref, start, frames in zip(refs, STARTS, PIECES):
        ref[...] = x_ref[start * SPOTS : (start + frames) * SPOTS]


def own_kernel(*refs):
    mod_ref, weight_ref, x_hbm, wq_hbm = refs[:4]
    stored_hbm = refs[4:11]
    share_ref, x_ref, q_ref, kv_ref = refs[11:15]
    stored = refs[15:22]
    wq_ref, sem = refs[22:]
    copies = [
        pltpu.make_async_copy(src, dst, sem.at[i])
        for i, (src, dst) in enumerate(
            zip((x_hbm, wq_hbm) + stored_hbm, (x_ref, wq_ref) + stored)
        )
    ]
    for copy in copies:
        copy.start()

    count = weight_ref.shape[1]
    strip = lax.axis_index("lon")
    weights = weight_ref[...].astype(jnp.float32)
    spot = lax.broadcasted_iota(jnp.int32, weights.shape, 1)
    here = jnp.sum(jnp.where(spot == strip, weights, 0.0), axis=1, keepdims=True)
    prior = jnp.sum(
        jnp.where(spot == lax.rem(strip + count - 1, count), weights, 0.0), axis=1, keepdims=True
    )
    near = jnp.where(lax.rem(strip, 2) == 0, here, prior)
    share_ref[...] = jnp.broadcast_to(near / (here + prior), share_ref.shape)

    copies[0].wait()
    n = normed(x_ref[...].astype(jnp.float32), mod_ref[0:1], mod_ref[1:2]).astype(jnp.bfloat16)
    copies[1].wait()
    q_ref[...] = scaled(project(n, wq_ref))
    for i in range(2):
        copies[2 + i].wait()
        kv_ref[:, i * HW : (i + 1) * HW] = project(n, stored[i])
    for copy in copies[4:]:
        copy.wait()


def quad_lanes(quad):
    wide = HW // 2
    return slice(quad * wide, (quad + 1) * wide), slice(HW + quad * wide, HW + (quad + 1) * wide)


def frame_rows(f):
    return slice(f * SPOTS, (f + 1) * SPOTS)


def near_kernel(x_ref, share_ref, q_ref, kv_ref, mod_ref, wk_ref, wv_ref, part_ref, raised_ref, stats_ref):
    n = normed(x_ref[...].astype(jnp.float32), mod_ref[0:1], mod_ref[1:2]).astype(jnp.bfloat16)
    k_near, v_near = project(n, wk_ref), project(n, wv_ref)
    units = [(f, quad) for f in range(F) for quad in range(2)]
    for first in range(0, len(units), SPACE_TOGETHER):
        batch = units[first : first + SPACE_TOGETHER]
        scored = []
        for f, quad in batch:
            lanes, after = quad_lanes(quad)
            at = frame_rows(f)
            keys = jnp.concatenate([kv_ref[at, lanes], k_near[at, lanes]], axis=0)
            stacked = spread_heads(q_ref[at, lanes], HEADS // 2)
            scored.append(raise_scores(keys, stacked, SPOTS))
        for (f, quad), (own, other) in zip(batch, scored):
            lanes, after = quad_lanes(quad)
            at = frame_rows(f)
            unit = 2 * f + quad
            raised_ref[unit] = own[0]
            stats_ref[unit, 0:1] = own[1]
            stats_ref[unit, 1:2] = own[2]
            part_ref[at, lanes] = mix_values(
                [own[0], other[0]],
                window_factors(share_ref[f : f + 1], own[1:], other[1:]),
                [kv_ref[at, after], v_near[at, lanes]],
                SPOTS,
                HEADS // 2,
            )


def space_kernel(start, frames, *refs):
    far_ref, part_ref, raised_ref, stats_ref, share_ref, x_ref, q_ref, kv_ref = refs[:8]
    mod_ref, wk_ref, wv_ref, wo_ref, wkt_ref, wvt_ref = refs[8:14]
    mixed_ref, n_ref, kvt_ref = refs[14:]
    rows = frames * SPOTS
    far = far_ref[...]
    if PAD and rows < LANES:
        far = jnp.concatenate([far, far[: LANES - rows]], axis=0)
    n = normed(far.astype(jnp.float32), mod_ref[0:1], mod_ref[1:2]).astype(jnp.bfloat16)
    k_far, v_far = project(n, wk_ref), project(n, wv_ref)
    units = [(f, quad) for f in range(frames) for quad in range(2)]
    blended = {}
    for first in range(0, len(units), SPACE_TOGETHER):
        batch = units[first : first + SPACE_TOGETHER]
        scored = []
        for f, quad in batch:
            lanes, after = quad_lanes(quad)
            stacked = spread_heads(q_ref[frame_rows(start + f), lanes], HEADS // 2)
            scored += raise_scores(k_far[frame_rows(f), lanes], stacked, SPOTS)
        for (f, quad), other in zip(batch, scored):
            lanes, after = quad_lanes(quad)
            own = frame_rows(start + f)
            unit = 2 * (start + f) + quad
            stats = (stats_ref[unit, 0:1], stats_ref[unit, 1:2])
            share = 1.0 - share_ref[start + f : start + f + 1]
            mix = mix_values(
                [raised_ref[unit], other[0]],
                window_factors(share, stats, other[1:]),
                [kv_ref[own, after], v_far[frame_rows(f), lanes]],
                SPOTS,
                HEADS // 2,
            )
            blended[f, quad] = (part_ref[own, lanes] + mix).astype(jnp.bfloat16)
    blended = jnp.concatenate(
        [
            jnp.concatenate([blended[f, quad] for quad in range(2)], axis=1)
            for f in range(frames)
        ],
        axis=0,
    )
    here = slice(start * SPOTS, (start + frames) * SPOTS)
    branch = f32dot(blended, wo_ref[...])
    mixed = (x_ref[here].astype(jnp.float32) + mod_ref[2:3] * branch).astype(jnp.bfloat16)
    mixed_ref[...] = mixed
    n = normed(mixed.astype(jnp.float32), mod_ref[3:4], mod_ref[4:5])
    n = n.reshape(frames, GROUPS, GROUP, D).transpose(1, 0, 2, 3).reshape(rows, D)
    n = n.astype(jnp.bfloat16)
    kvt_ref[:, :HW] = project(n, wkt_ref)
    kvt_ref[:, HW:] = project(n, wvt_ref)
    n_ref[...] = n


def time_setup():
    rows = F * GROUP
    key_spot = lax.broadcasted_iota(jnp.int32, (rows, LANES), 0) % GROUP
    query_spot = lax.broadcasted_iota(jnp.int32, (rows, LANES), 1) % GROUP
    bias = jnp.where(key_spot == query_spot, 0.0, NEG)
    group = lax.axis_index("frames")
    inner = jnp.logical_and(group > 0, group < lax.axis_size("frames") - 1)
    return bias, jnp.where(inner, 0.5, 0.0)


def rows_of(refs, g, lanes):
    return jnp.concatenate(
        [
            ref[g * frames * GROUP : (g + 1) * frames * GROUP, lanes]
            for ref, frames in zip(refs, PIECES)
        ],
        axis=0,
    )


def pair_lanes(pair):
    return slice(pair * LANES, (pair + 1) * LANES), slice(
        HW + pair * LANES, HW + (pair + 1) * LANES
    )


def mate_kernel(*refs):
    count = len(PIECES)
    wq_ref = refs[0]
    n_refs, own_refs, mate_refs = (refs[1 + i * count : 1 + (i + 1) * count] for i in range(3))
    q_ref, part_ref, raised_ref, stats_ref = refs[1 + 3 * count :]
    bias, paired = time_setup()
    n = F * GROUP
    q = scaled(project(jnp.concatenate([ref[...] for ref in n_refs], axis=0), wq_ref))
    for g in range(GROUPS):
        q_ref[g * n : (g + 1) * n] = jnp.concatenate(
            [
                q[start * SPOTS + g * frames * GROUP : start * SPOTS + (g + 1) * frames * GROUP]
                for start, frames in zip(STARTS, PIECES)
            ],
            axis=0,
        )
    units = [(g, pair) for g in range(GROUPS) for pair in range(HEADS // 2)]
    for first in range(0, len(units), TOGETHER):
        batch = units[first : first + TOGETHER]
        scored = []
        for g, pair in batch:
            lanes, after = pair_lanes(pair)
            stacked = spread_heads(q_ref[g * n : (g + 1) * n, lanes], 2)
            keys = jnp.concatenate(
                [rows_of(own_refs, g, lanes), rows_of(mate_refs, g, lanes)], axis=0
            )
            scored.append(raise_scores(keys, stacked, n, bias))
        for (g, pair), (own, other) in zip(batch, scored):
            lanes, after = pair_lanes(pair)
            unit = g * (HEADS // 2) + pair
            raised_ref[unit] = own[0]
            stats_ref[unit, 0:1] = own[1]
            stats_ref[unit, 1:2] = own[2]
            part_ref[g * n : (g + 1) * n, lanes] = mix_values(
                [own[0], other[0]],
                window_factors(1.0 - paired, own[1:], other[1:]),
                [rows_of(own_refs, g, after), rows_of(mate_refs, g, after)],
                n,
                2,
            )


def cross_kernel(mod_ref, wo_ref, q_ref, part_ref, raised_ref, stats_ref, *refs):
    count = len(PIECES)
    own_refs, cross_refs, mixed_refs = (refs[i * count : (i + 1) * count] for i in range(3))
    out_hbm, out_ref, sem = refs[3 * count :]
    bias, paired = time_setup()
    n = F * GROUP
    copies = []
    per = GROUPS // 2
    pairs = range(HEADS // 2)

    def score(half):
        scored = {}
        for g in range(half * per, (half + 1) * per):
            for pair in pairs:
                lanes, _ = pair_lanes(pair)
                stacked = spread_heads(q_ref[g * n : (g + 1) * n, lanes], 2)
                scored[g, pair] = raise_scores(rows_of(cross_refs, g, lanes), stacked, n, bias)[0]
        return scored

    scored = {}
    if AHEAD:
        for half in range(2):
            scored.update(score(half))
    for half in range(2):
        if not AHEAD:
            scored = score(half)
        rows = []
        for g in range(half * per, (half + 1) * per):
            row = []
            for pair in pairs:
                lanes, after = pair_lanes(pair)
                unit = g * (HEADS // 2) + pair
                other = scored[g, pair]
                stats = (stats_ref[unit, 0:1], stats_ref[unit, 1:2])
                mix = mix_values(
                    [raised_ref[unit], other[0]],
                    window_factors(paired, stats, other[1:]),
                    [rows_of(own_refs, g, after), rows_of(cross_refs, g, after)],
                    n,
                    2,
                )
                row.append((part_ref[g * n : (g + 1) * n, lanes] + mix).astype(jnp.bfloat16))
            rows.append(jnp.concatenate(row, axis=1))
        branch = mod_ref[5:6] * f32dot(jnp.concatenate(rows, axis=0), wo_ref[...])
        branch = branch.reshape(per, F, GROUP, D)
        spots = pl.ds(half * per, per)
        for mixed_ref, start, frames in zip(mixed_refs, STARTS, PIECES):
            for f in range(frames):
                for i in range(per):
                    at = f * SPOTS + (half * per + i) * GROUP
                    mixed = mixed_ref[at : at + GROUP].astype(jnp.float32)
                    out_ref[start + f, half * per + i] = (mixed + branch[i, start + f]).astype(
                        jnp.bfloat16
                    )
        copies.append(
            pltpu.make_async_copy(out_ref.at[:, spots], out_hbm.at[:, spots], sem.at[half])
        )
        copies[-1].start()
    for copy in copies:
        copy.wait()


def body(
    latents,
    window_weight,
    modulation,
    query_spatial,
    key_spatial,
    value_spatial,
    out_spatial,
    query_temporal,
    key_temporal,
    value_temporal,
    out_temporal,
):
    strips = lax.axis_size("lon")
    groups = lax.axis_size("frames")
    bf = jnp.bfloat16
    shape = jax.ShapeDtypeStruct
    params = pltpu.CompilerParams

    def keep(array):
        return pltpu.with_memory_space_constraint(array, pltpu.HBM)

    x = latents.reshape(TOK, D)
    near_pairs = [(i, i ^ 1) for i in range(strips)]
    far_pairs = [(i, (i + (1 if i % 2 else -1)) % strips) for i in range(strips)]
    mates = [(i, i ^ 1) for i in range(groups)]
    crossing = []
    for i in range(groups):
        for s in range(strips):
            if i in (0, groups - 1):
                crossing.append((i * strips + s, i * strips + (s ^ 1)))
            else:
                partner = i + 1 if i % 2 else i - 1
                crossing.append((i * strips + s, partner * strips + s))

    near = lax.ppermute(x, "lon", near_pairs)
    pieces = pl.pallas_call(
        split_kernel,
        out_shape=[shape((n * SPOTS, D), bf) for n in PIECES],
        in_specs=[VM],
        out_specs=[VM] * len(PIECES),
        compiler_params=params(vmem_limit_bytes=4 * MIB),
        name="split",
    )(x)
    far = []
    for piece in pieces:
        far.append(lax.ppermute(piece, "lon", far_pairs))

    wide, tall = shape((D, HW), bf), shape((HW, D), bf)
    stored = pl.pallas_call(
        own_kernel,
        out_shape=[shape((F, LANES), jnp.float32), shape((TOK, D), bf)]
        + [shape((TOK, HW), bf), shape((TOK, D), bf)]
        + [wide, wide, tall, wide, wide, wide, tall],
        in_specs=[VM] * 2 + [HBM] * 9,
        out_specs=[VM] * 11,
        scratch_shapes=[pltpu.VMEM((D, HW), bf), pltpu.SemaphoreType.DMA((9,))],
        compiler_params=params(vmem_limit_bytes=24 * MIB),
        name="own",
    )(
        modulation,
        window_weight,
        *map(
            keep,
            (
                x,
                query_spatial,
                key_spatial,
                value_spatial,
                out_spatial,
                key_temporal,
                value_temporal,
                query_temporal,
                out_temporal,
            ),
        ),
    )
    share, own_x, q, kv = stored[:4]
    weights = stored[4:9]
    space_units = 2 * F
    near_parts = pl.pallas_call(
        near_kernel,
        out_shape=[
            shape((TOK, HW), jnp.float32),
            shape((space_units, SPOTS, LANES), jnp.float32),
            shape((space_units, 8, LANES), jnp.float32),
        ],
        in_specs=[VM] * 7,
        out_specs=[VM] * 3,
        compiler_params=params(vmem_limit_bytes=16 * MIB),
        name="near",
    )(near, share, q, kv, modulation, *weights[:2])
    time_args = []
    for i, (start, frames) in enumerate(zip(STARTS, PIECES)):
        rows = frames * SPOTS
        args = (far[i], *near_parts, share, own_x, q, kv, modulation, *weights)
        mixed, nt, kvt = pl.pallas_call(
            functools.partial(space_kernel, start, frames),
            out_shape=[shape((rows, D), bf)] * 3,
            in_specs=[VM] * len(args),
            out_specs=[VM] * 3,
            compiler_params=params(vmem_limit_bytes=20 * MIB),
        )(*args)
        cross = lax.ppermute(kvt, ("frames", "lon"), crossing)
        mate = lax.ppermute(kvt, "frames", mates)
        time_args.append((nt, kvt, mate, cross, mixed))

    nts, kvts, mate_kvs, cross_kvs, mixeds = zip(*time_args)
    units = GROUPS * HEADS // 2
    parts = pl.pallas_call(
        mate_kernel,
        out_shape=[
            shape((TOK, HW), bf),
            shape((TOK, HW), jnp.float32),
            shape((units, F * GROUP, LANES), jnp.float32),
            shape((units, 8, LANES), jnp.float32),
        ],
        in_specs=[VM] * (1 + 3 * len(PIECES)),
        out_specs=[VM] * 4,
        compiler_params=params(vmem_limit_bytes=12 * MIB),
        name="timea",
    )(stored[9], *nts, *kvts, *mate_kvs)
    out_shape = (F, GROUPS, GROUP, D)
    out = pl.pallas_call(
        cross_kernel,
        out_shape=shape(out_shape, bf),
        in_specs=[VM] * (6 + 3 * len(PIECES)),
        out_specs=HBM,
        scratch_shapes=[pltpu.VMEM(out_shape, bf), pltpu.SemaphoreType.DMA((2,))],
        compiler_params=params(vmem_limit_bytes=16 * MIB),
        name="timeb",
    )(modulation, stored[10], *parts, *kvts, *cross_kvs, *mixeds)
    return out.reshape(latents.shape)


def solution(mesh):
    return jax.shard_map(
        body,
        mesh=mesh,
        in_specs=(P("frames", None, "lon", None), P("frames", None)) + (P(),) * 9,
        out_specs=P("frames", None, "lon", None),
        check_vma=False,
    )
```
